32 devices in a mesh: shard: 4 (over z), rep: 8 (over y, x, core).
Axes of the slice: x: 2, y: 2, z: 4, core: 2. Of those that a mesh axis runs over, the one named last changes fastest.
Arguments:
- inputs: float32 [64, 320, 1024], P(('shard', 'rep')), may hold values from -6 to 6
- counts: int32 [64], P(('shard', 'rep')), may hold values from 64 to 320, as said below
- w_qkv: float32 [1024, 3072], P('shard'), may hold values from -0.1875 to 0.1875
- w_out: float32 [1024, 1024], P('shard'), may hold values from -0.75 to 0.75
- w_up: float32 [1024, 4096], P('shard'), may hold values from -0.1875 to 0.1875
- w_down: float32 [4096, 1024], P('shard'), may hold values from -0.09375 to 0.09375
- vectors: float32 [12288], P('shard'), may hold values from -1.2 to 1.8
- cotangent: float32 [64, 320, 1024], P(('shard', 'rep')), may hold values from -6 to 6
Outputs:
- outputs: float32 [64, 320, 1024], P(('shard', 'rep'))
- grad_inputs: float32 [64, 320, 1024], P(('shard', 'rep'))
- grad_qkv: float32 [1024, 3072], P('shard')
- grad_out: float32 [1024, 1024], P('shard')
- grad_up: float32 [1024, 4096], P('shard')
- grad_down: float32 [4096, 1024], P('shard')
- grad_vectors: float32 [12288], P('shard')
The draws below stay inside these ranges and needn't reach their ends.
Inputs may be any that keep to these rules, and one draw needn't show every extreme that they name: Slots 0 to counts[s] - 1 of sequence s are kept; some sequence keeps all 320, some only the 64 buffer slots.
All inputs are finite; a program needn't handle non-finite values.
Results may differ from the reference program's by a relative error of at most 0.014.
Values may be sent and summed in bfloat16 or wider, within the bound.
No kernel may reach another device: no remote copies, remote signals or barrier semaphores. Data moves between devices by JAX's collectives and lax.ppermute only.
A program may use at most 256 MiB of HBM per device.

```python
import jax
import jax.numpy as jnp
from jax import lax

D = 1024
HEADS = 16
HEAD_DIM = 64
FF = 4096
SLOTS = 320
BUFFER = 64
SEQ_DEV = 2
SEQS = 64
N_SHARD = 4


def draw_counts(key, part):
    drawn = jax.random.randint(key, (SEQS,), BUFFER, SLOTS + 1)
    chosen = jax.random.randint(jax.random.fold_in(key, 7), (), 0, SEQS)
    offset = jax.random.randint(jax.random.fold_in(key, 11), (), 1, SEQS)
    chosen_low = (chosen + offset) % SEQS
    positions = jnp.arange(SEQS)
    drawn = jnp.where(positions == chosen_low, BUFFER, drawn)
    drawn = jnp.where(positions == chosen, SLOTS, drawn)
    return drawn.astype(jnp.int32)


def draw_vectors(key, part):
    noise = jnp.clip(jax.random.normal(key, (12, D), jnp.float32), -4.0, 4.0)
    row_number = jnp.arange(12)[:, None]
    is_gain = (row_number == 0) | (row_number == 5)
    return jnp.where(is_gain, 1.0 + 0.2 * noise, 0.3 * noise).reshape(12 * D).astype(jnp.float32)


def steps_of(rng, dims, cuts, smallest, high):
    gain, own = 1.0, jax.random.fold_in(rng, 6)
    for dim, blocks in cuts:
        steps = jnp.exp(jax.random.uniform(jax.random.fold_in(own, dim), (blocks,), jnp.float32, smallest / len(cuts), high / len(cuts)))
        gain = gain * jnp.repeat(steps, dims[dim] // blocks).reshape([-1 if axis == dim else 1 for axis in range(len(dims))])
    return gain


def gaussian(stream_key, shape, width, reach, shards=(), held_as=jnp.bfloat16):
    values = jax.random.normal(stream_key, shape, jnp.float32) * width
    if len(shards) > 0:
        values = steps_of(stream_key, shape, shards, -0.22, 0.18) * values
    return jnp.clip(values, min=-reach, max=reach).astype(held_as)


def setup_inputs(seed: int = 0) -> dict:
    splits = jax.random.split(jax.random.key(seed), 9)
    inputs = gaussian(splits[0], (SEQS, SLOTS, D), 1.0, 6.0, ((0, 32),), jnp.float32)
    counts = draw_counts(jax.random.fold_in(splits[8], 71), 0)
    w_qkv = gaussian(splits[2], (D, 3 * D), D ** -0.5, 0.1875, ((0, 4),), jnp.float32)
    w_out = gaussian(splits[3], (D, D), (D // 16) ** -0.5, 0.75, ((0, 4),), jnp.float32)
    w_up = gaussian(splits[4], (D, FF), D ** -0.5, 0.1875, ((0, 4),), jnp.float32)
    w_down = gaussian(splits[5], (FF, D), FF ** -0.5, 0.09375, ((0, 4),), jnp.float32)
    vectors = draw_vectors(jax.random.fold_in(splits[8], 71), 0)
    cotangent = gaussian(splits[7], (SEQS, SLOTS, D), 1.0, 6.0, ((0, 32),), jnp.float32)
    return dict(inputs=inputs, counts=counts, w_qkv=w_qkv, w_out=w_out, w_up=w_up, w_down=w_down, vectors=vectors, cotangent=cotangent)


@jax.custom_vjp
def low(v):
    return lax.optimization_barrier(v.astype(jnp.bfloat16)).astype(jnp.float32)

@jax.custom_vjp
def low_back(v):
    return v

def low_keep(v):
    return (low(v), None)

def low_pass(kept, grad):
    return (grad,)

def back_keep(v):
    return (v, None)

def back_low(kept, grad):
    return (low(grad),)
low.defvjp(low_keep, low_pass)
low_back.defvjp(back_keep, back_low)
layer_eps = 1e-06

def matmul(left, right):
    return jnp.dot(left, right, precision=lax.Precision.HIGHEST, preferred_element_type=jnp.float32)

def norm_rows(source, row_gain, row_shift):
    row_mean = lax.optimization_barrier(jnp.mean(source, axis=-1, keepdims=True))
    centred = source - row_mean
    row_var = lax.optimization_barrier(jnp.mean(centred * centred, axis=-1, keepdims=True))
    return centred * lax.rsqrt(row_var + layer_eps) * row_gain + row_shift

def forward(source, counts, w_qkv, w_out, w_up, w_down, vectors):
    seq_count = source.shape[0]
    params = low(vectors).reshape(12, D)
    gain_one = params[0]
    shift_one = params[1]
    bias_query = params[2]
    bias_value = params[3]
    bias_out = params[4]
    gain_two = params[5]
    shift_two = params[6]
    bias_down = params[7]
    bias_hidden = params[8:].reshape(FF)
    valid_slots = jnp.arange(SLOTS, dtype=jnp.int32)[None, :] < counts[:, None]
    flat_rows = source.reshape(-1, D)
    normed_one = low(norm_rows(flat_rows, gain_one, shift_one))
    bias_qkv = jnp.concatenate([bias_query, jnp.zeros_like(bias_query), bias_value])
    projected = low(low_back(matmul(normed_one, low(w_qkv)) + bias_qkv))
    projected = projected.reshape(seq_count, SLOTS, 3, HEADS, HEAD_DIM)
    queries = projected[:, :, 0]
    key_heads = projected[:, :, 1]
    value_heads = projected[:, :, 2]
    scaled = jnp.einsum('bqhd,bkhd->bhqk', queries, key_heads, precision=lax.Precision.HIGHEST) * HEAD_DIM ** (-0.5)
    scores = jnp.where(valid_slots[:, None, None, :], low_back(scaled), -1e+30)
    row_top = lax.optimization_barrier(jnp.max(scores, axis=-1, keepdims=True))
    exp_scores = jnp.exp(scores - row_top)
    attn_weights = low(exp_scores / lax.optimization_barrier(jnp.sum(exp_scores, axis=-1, keepdims=True)))
    attended = jnp.einsum('bhqk,bkhd->bqhd', attn_weights, value_heads, precision=lax.Precision.HIGHEST)
    attended = low(low_back(attended.reshape(-1, D)))
    middle = flat_rows + low_back(matmul(attended, low(w_out)) + bias_out)
    normed_two = low(norm_rows(middle, gain_two, shift_two))
    hidden = low_back(matmul(normed_two, low(w_up)) + bias_hidden)
    activated = low(jax.nn.gelu(hidden, approximate=False))
    result = middle + low_back(matmul(activated, low(w_down)) + bias_down)
    keep_rows = valid_slots.reshape(-1, 1).astype(source.dtype)
    return (result * keep_rows).reshape(seq_count, SLOTS, D)

def reference(inputs, counts, w_qkv, w_out, w_up, w_down, vectors, cotangent):
    group_size = SEQ_DEV * N_SHARD
    block_count = SEQS // group_size

    def one_block(totals, pieces):
        block_inputs, block_counts, block_cotangent = pieces

        def block_forward(source, first, second, third, fourth, packed):
            return forward(source, block_counts, first, second, third, fourth, packed)
        block_outputs, pullback = jax.vjp(block_forward, block_inputs, w_qkv, w_out, w_up, w_down, vectors)
        gradients = pullback(block_cotangent)
        totals = tuple((running + addend for running, addend in zip(totals, gradients[1:])))
        return (totals, (block_outputs, gradients[0]))
    initial = (jnp.zeros_like(w_qkv), jnp.zeros_like(w_out), jnp.zeros_like(w_up), jnp.zeros_like(w_down), jnp.zeros_like(vectors))
    totals, (all_outputs, all_inputs_grad) = lax.scan(one_block, initial, (inputs.reshape(block_count, group_size, SLOTS, D), counts.reshape(block_count, group_size), cotangent.reshape(block_count, group_size, SLOTS, D)))
    return (all_outputs.reshape(SEQS, SLOTS, D), all_inputs_grad.reshape(SEQS, SLOTS, D), totals[0], totals[1], totals[2], totals[3], totals[4])
```

```python
import functools

import jax
import jax.numpy as jnp
from jax import lax
from jax.experimental import pallas as pl
from jax.experimental.pallas import tpu as pltpu
from jax.sharding import PartitionSpec as P

HEAD_DIM = 64
EPS = 1e-06
LOW = jnp.bfloat16
F32 = jnp.float32
NZ = 4
NP = 8
CORE, BITX, BITY = 1, 2, 4
MIB = 1 << 20


def nt_dot(left, right):
    return lax.dot_general(
        left, right, (((1,), (1,)), ((), ())), preferred_element_type=F32
    )


def nn_dot(left, right):
    return jnp.dot(left, right, preferred_element_type=F32)


def row_stats(rows):
    mean = jnp.mean(rows, axis=-1, keepdims=True)
    centred = rows - mean
    inv = lax.rsqrt(jnp.mean(centred * centred, axis=-1, keepdims=True) + EPS)
    return centred * inv, inv


class Links:
    def __init__(self, n_rep):
        self.n_rep = n_rep

    def rep(self, value, bit, name):
        with jax.named_scope(name):
            return lax.ppermute(value, "rep", [(i, i ^ bit) for i in range(self.n_rep)])

    def zed(self, value, bit, name):
        with jax.named_scope(name):
            return lax.ppermute(value, "shard", [(i, i ^ bit) for i in range(NZ)])


FIRST = (BITX, BITY)
SECOND = (BITY, BITX)
BOTH = BITX | BITY


def gather_parts(links, own8, r, name):
    kb, nb = own8.shape[1:]
    mine = lax.dynamic_index_in_dim(own8, r, 0, keepdims=False).reshape(2, kb // 2, nb)
    one = links.zed(mine, 1, name + "_z1")
    pair = links.zed(jnp.stack([mine, one]), 2, name + "_z2")
    held = []
    for h in range(2):
        base = jnp.concatenate([one[h][None], pair[:, h]])
        near = links.rep(base, FIRST[h], f"{name}_a{h}")
        far = links.rep(jnp.stack([base, near]), SECOND[h], f"{name}_b{h}")
        held.append(jnp.concatenate([base[None], near[None], far]))
    held = jnp.stack(held)
    return held, links.rep(held, CORE, name + "_c")


HELD = ((0, BITX, BITY, BOTH), (0, BITY, BITX, BOTH))


def sum_low(*terms):
    total = terms[0].astype(F32)
    for term in terms[1:]:
        total = total + term.astype(F32)
    return total


ORDER = (((1, 3), (0, 2)), ((2, 3), (0, 1)))


def reduce_parts(links, keep, send, flip, name):
    recv = links.rep(send, CORE, name + "_c")
    bases = []
    for h in range(2):
        sent_idx, kept_idx = ORDER[h]
        own = (keep[h], recv[h])
        sent = sum_low(*[jnp.stack([a[i] for i in sent_idx]) for a in own]).astype(LOW)
        got1 = links.rep(sent, FIRST[h], f"{name}_a{h}")
        other = kept_idx[1]
        sent = sum_low(own[0][other], own[1][other], got1[1]).astype(LOW)
        got2 = links.rep(sent, SECOND[h], f"{name}_b{h}")
        bases.append((own[0][0], own[1][0], got1[0], got2))
    sent = jnp.stack([sum_low(*[b[2:4] for b in base]).astype(LOW) for base in bases])
    got3 = links.zed(sent, 2, name + "_z2")
    sent = jnp.stack(
        [sum_low(*[b[1] for b in base], got3[h, 1]).astype(LOW) for h, base in enumerate(bases)]
    )
    got4 = links.zed(sent, 1, name + "_z1")
    total = jnp.stack(
        [
            sum_low(*[b[0] for b in base], got3[h, 0], got4[h]).astype(LOW)
            for h, base in enumerate(bases)
        ]
    )
    bit = NP
    while bit < links.n_rep:
        total = sum_low(total, links.rep(total, bit, f"{name}_r{bit}")).astype(LOW)
        bit *= 2
    near = links.rep(total, FIRST[flip], name + "_d")
    far = links.rep(jnp.stack([total, near]), SECOND[flip], name + "_e")
    held = jnp.concatenate([total[None], near[None], far])
    return held, links.rep(held, CORE, name + "_f")


HBM = pl.BlockSpec(memory_space=pltpu.HBM)
WHOLE = pl.BlockSpec(memory_space=pltpu.VMEM)
SCALARS = pl.BlockSpec(memory_space=pltpu.SMEM)


class Weight:
    def __init__(self, own, held, other, cols=None):
        self.arrays = [own, held, other]
        self.kb = own.shape[1]
        self.cols = slice(0, own.shape[2]) if cols is None else cols
        self.nb = self.cols.stop - self.cols.start

    def start(self, sc, refs, place, sems):
        z, r = sc[0], sc[1]
        own, held, other = refs
        half = self.kb // 2
        for j in range(NP):
            part = r ^ j
            copies = [(own.at[part, :, self.cols], place(z, part, 0, self.kb))]
            source = other if j & CORE else held
            for h in range(2):
                index = HELD[h].index(j & ~CORE)
                for k in range(1, NZ):
                    copies.append(
                        (
                            source.at[h, index, k - 1, :, self.cols],
                            place(z ^ k, part, h * half, half),
                        )
                    )
            for src, dst in copies:
                pltpu.make_async_copy(src, dst, sems.at[j]).start()

    def rows_first(self, w_ref):
        def place(zc, part, row, rows):
            return w_ref.at[part, zc, pl.ds(row, rows)]

        return place

    def flat(self, w_ref):
        def place(zc, part, row, rows):
            return w_ref.at[
                pl.ds(pl.multiple_of(zc * self.kb + row, 128), rows),
                pl.ds(pl.multiple_of(part * self.nb, self.nb), self.nb),
            ]

        return place


def wait_for(ref, sem):
    pltpu.make_async_copy(ref, ref, sem).wait()


def call(body, name, outs, in_specs, scratch, args, flops, limit, out_specs=None, grid=None):
    moved = sum(a.size * a.dtype.itemsize for a in args) + sum(
        o.size * o.dtype.itemsize for o in outs
    )
    extra = {} if grid is None else {"grid": grid}
    return pl.pallas_call(
        body,
        out_shape=outs,
        in_specs=in_specs,
        out_specs=[WHOLE] * len(outs) if out_specs is None else out_specs,
        scratch_shapes=scratch,
        compiler_params=pltpu.CompilerParams(vmem_limit_bytes=limit * MIB),
        cost_estimate=pl.CostEstimate(
            flops=int(flops), bytes_accessed=int(moved), transcendentals=0
        ),
        name=name,
        **extra,
    )(*args)


def shaped(shape, dtype):
    return jax.ShapeDtypeStruct(shape, dtype)


def project_qkv(sc, rows, params, weight):
    n_rows, width = rows.shape
    nb = weight.nb
    third = nb // 3

    def body(sc_ref, x_ref, p_ref, own, held, other, a_ref, y_ref, w_ref, sems):
        r = sc_ref[1]
        weight.start(sc_ref, (own, held, other), weight.rows_first(w_ref), sems)
        xh, _ = row_stats(x_ref[...])
        a_ref[...] = (xh * p_ref[0:1, :] + p_ref[1:2, :]).astype(LOW)

        @pl.loop(0, NP)
        def _(j):
            part = r ^ j
            wait_for(w_ref.at[part], sems.at[j])
            y = nn_dot(a_ref[...], w_ref[part].reshape(width, nb))
            first = pl.ds(pl.multiple_of(part * third, third), third)
            second = pl.ds(pl.multiple_of(part * third + width, third), third)
            last = pl.ds(pl.multiple_of(part * third + 2 * width, third), third)
            y_ref[:, first] = (y[:, :third] + p_ref[2:3, first]).astype(LOW)
            y_ref[:, second] = y[:, third : 2 * third].astype(LOW)
            y_ref[:, last] = (y[:, 2 * third :] + p_ref[3:4, first]).astype(LOW)

    return call(
        body,
        "project_qkv",
        [shaped((n_rows, width), LOW), shaped((n_rows, 3 * width), LOW)],
        [SCALARS, WHOLE, WHOLE, HBM, HBM, HBM],
        [pltpu.VMEM((NP, NZ, weight.kb, nb), LOW), pltpu.SemaphoreType.DMA((NP,))],
        [sc, rows, params] + weight.arrays,
        2 * n_rows * width * 3 * width,
        28,
    )


def attend(counts, qkv, seqs):
    n_rows, wide = qkv.shape
    width = wide // 3
    slots = n_rows // seqs
    pairs = width // 128

    def body(counts_ref, q_ref, k_ref, v_ref, o_ref):
        count = counts_ref[pl.program_id(1)]
        low_half = lax.broadcasted_iota(jnp.int32, (slots, 128), 1) < HEAD_DIM
        kept = lax.broadcasted_iota(jnp.int32, (slots, slots), 1) < count
        q = q_ref[...] * jnp.asarray(HEAD_DIM**-0.5, LOW)
        k, v = k_ref[...], v_ref[...]
        zero = jnp.zeros_like(q)
        parts = []
        for chosen in (jnp.where(low_half, q, zero), jnp.where(low_half, zero, q)):
            s = jnp.where(kept, nt_dot(chosen, k), -1e30)
            e = jnp.exp(s - jnp.max(s, axis=-1, keepdims=True))
            inv = 1.0 / jnp.sum(e, axis=-1, keepdims=True)
            parts.append(nn_dot((e * inv).astype(LOW), v))
        o_ref[...] = jnp.where(low_half, parts[0], parts[1]).astype(LOW)

    def at(offset):
        return pl.BlockSpec((slots, 128), lambda p, s: (s, p + offset))

    return call(
        body,
        "attend",
        [shaped((n_rows, width), LOW)],
        [SCALARS, at(0), at(pairs), at(2 * pairs)],
        [],
        [counts, qkv, qkv, qkv],
        4 * n_rows * slots * width,
        16,
        [at(0)],
        (pairs, seqs),
    )[0]


def attend_back(counts, qkv, d_out, seqs):
    n_rows, wide = qkv.shape
    width = wide // 3
    slots = n_rows // seqs
    pairs = width // 128

    def body(counts_ref, q_ref, k_ref, v_ref, do_ref, dq_ref, dk_ref, dv_ref, bq_ref, bv_ref):
        seq = pl.program_id(1)
        count = counts_ref[seq]
        low_half = lax.broadcasted_iota(jnp.int32, (slots, 128), 1) < HEAD_DIM
        kept = lax.broadcasted_iota(jnp.int32, (slots, slots), 0) < count
        q = q_ref[...] * jnp.asarray(HEAD_DIM**-0.5, LOW)
        k, v, do = k_ref[...], v_ref[...], do_ref[...]
        zero = jnp.zeros_like(q)
        dq, dk, dv = [], [], []
        for side in range(2):
            def only(a):
                return jnp.where(low_half, a, zero) if side == 0 else jnp.where(low_half, zero, a)

            q_one, do_one = only(q), only(do)
            s = jnp.where(kept, nt_dot(k, q_one), -1e30)
            e = jnp.exp(s - jnp.max(s, axis=0, keepdims=True))
            p = e * (1.0 / jnp.sum(e, axis=0, keepdims=True))
            dp = nt_dot(v, do_one)
            inner = jnp.sum(p * dp, axis=0, keepdims=True)
            ds = (p * (dp - inner)).astype(LOW)
            dv.append(nn_dot(p.astype(LOW), do_one))
            dk.append(nn_dot(ds, q_one))
            dq.append(
                lax.dot_general(
                    ds, only(k), (((0,), (0,)), ((), ())), preferred_element_type=F32
                )
            )
        dq_all = ((dq[0] + dq[1]) * HEAD_DIM**-0.5).astype(LOW)
        dv_all = (dv[0] + dv[1]).astype(LOW)
        dq_ref[...] = dq_all
        dk_ref[...] = (dk[0] + dk[1]).astype(LOW)
        dv_ref[...] = dv_all
        bq = jnp.sum(dq_all.astype(F32), axis=0, keepdims=True)
        bv = jnp.sum(dv_all.astype(F32), axis=0, keepdims=True)

        @pl.when(seq == 0)
        def _():
            bq_ref[...] = bq
            bv_ref[...] = bv

        @pl.when(seq != 0)
        def _():
            bq_ref[...] += bq
            bv_ref[...] += bv

    def at(offset):
        return pl.BlockSpec((slots, 128), lambda p, s: (s, p + offset))

    bias = pl.BlockSpec((1, 128), lambda p, s: (0, p))
    block = shaped((n_rows, width), LOW)
    return call(
        body,
        "attend_back",
        [block, block, block, shaped((1, width), F32), shaped((1, width), F32)],
        [SCALARS, at(0), at(pairs), at(2 * pairs), at(0)],
        [],
        [counts, qkv, qkv, qkv, d_out],
        10 * n_rows * slots * width,
        16,
        [at(0), at(0), at(0), bias, bias],
        (pairs, seqs),
    )


def project_out(sc, attended, rows, params, weight):
    n_rows, width = rows.shape
    nb = weight.nb

    def body(sc_ref, o_ref, x_ref, p_ref, own, held, other, h_ref, a_ref, w_ref, sems):
        weight.start(sc_ref, (own, held, other), weight.flat(w_ref), sems)
        for j in range(NP):
            wait_for(w_ref.at[:, j * nb : (j + 1) * nb], sems.at[j])
        h1 = x_ref[...] + nn_dot(o_ref[...], w_ref[...]) + p_ref[4:5, :]
        h_ref[...] = h1
        xh, _ = row_stats(h1)
        a_ref[...] = (xh * p_ref[5:6, :] + p_ref[6:7, :]).astype(LOW)

    return call(
        body,
        "project_out",
        [shaped((n_rows, width), F32), shaped((n_rows, width), LOW)],
        [SCALARS, WHOLE, WHOLE, WHOLE, HBM, HBM, HBM],
        [pltpu.VMEM((width, width), LOW), pltpu.SemaphoreType.DMA((NP,))],
        [sc, attended, rows, params] + weight.arrays,
        2 * n_rows * width * width,
        28,
    )


def expand(sc, normed, bias_hidden, weight):
    n_rows, width = normed.shape
    nb = weight.nb
    hidden = NP * nb

    def body(sc_ref, a_ref, b_ref, own, held, other, g_ref, gp_ref, w_ref, sems):
        r = sc_ref[1]
        weight.start(sc_ref, (own, held, other), weight.rows_first(w_ref), sems)

        @pl.loop(0, NP)
        def _(j):
            part = r ^ j
            wait_for(w_ref.at[part], sems.at[j])
            cols = pl.ds(pl.multiple_of(part * nb, nb), nb)
            u = nn_dot(a_ref[...], w_ref[part].reshape(width, nb)) + b_ref[:, cols]
            cdf = 0.5 + 0.5 * lax.erf(u * 0.7071067811865476)
            pdf = jnp.exp(u * u * -0.5) * 0.3989422804014327
            g_ref[:, cols] = (u * cdf).astype(LOW)
            gp_ref[:, cols] = (cdf + u * pdf).astype(LOW)

    return call(
        body,
        "expand",
        [shaped((n_rows, hidden), LOW), shaped((n_rows, hidden), LOW)],
        [SCALARS, WHOLE, WHOLE, HBM, HBM, HBM],
        [pltpu.VMEM((NP, NZ, weight.kb, nb), LOW), pltpu.SemaphoreType.DMA((NP,))],
        [sc, normed, bias_hidden] + weight.arrays,
        2 * n_rows * width * hidden,
        32,
    )


def contract(sc, active, middle, keep_rows, params, weight):
    n_rows, width = middle.shape
    kb = weight.kb

    def body(sc_ref, g_ref, h_ref, k_ref, p_ref, own, held, other, y_ref, w_ref, sems):
        r = sc_ref[1]
        weight.start(sc_ref, (own, held, other), weight.rows_first(w_ref), sems)
        y_ref[...] = h_ref[...] + p_ref[7:8, :]

        @pl.loop(0, NP)
        def _(j):
            part = r ^ j
            wait_for(w_ref.at[part], sems.at[j])
            g = jnp.concatenate(
                [
                    g_ref[:, pl.ds(pl.multiple_of((zc * NP + part) * kb, kb), kb)]
                    for zc in range(NZ)
                ],
                axis=1,
            )
            y_ref[...] += nn_dot(g, w_ref[part].reshape(NZ * kb, width))

        y_ref[...] = y_ref[...] * k_ref[...]

    return call(
        body,
        "contract",
        [shaped((n_rows, width), F32)],
        [SCALARS, WHOLE, WHOLE, WHOLE, WHOLE, HBM, HBM, HBM],
        [pltpu.VMEM((NP, NZ, kb, width), LOW), pltpu.SemaphoreType.DMA((NP,))],
        [sc, active, middle, keep_rows, params] + weight.arrays,
        2 * n_rows * width * active.shape[1],
        32,
    )[0]


def contract_back(sc, e2, slope, weight):
    n_rows, width = e2.shape
    kb = weight.kb
    hidden = slope.shape[1]

    def body(sc_ref, e_ref, gp_ref, own, held, other, du_ref, sum_ref, w_ref, sems):
        r = sc_ref[1]
        weight.start(sc_ref, (own, held, other), weight.rows_first(w_ref), sems)

        @pl.loop(0, NP)
        def _(j):
            part = r ^ j
            wait_for(w_ref.at[part], sems.at[j])
            dg = nt_dot(e_ref[...], w_ref[part].reshape(NZ * kb, width))
            for zc in range(NZ):
                cols = pl.ds(pl.multiple_of((zc * NP + part) * kb, kb), kb)
                du = (dg[:, zc * kb : (zc + 1) * kb] * gp_ref[:, cols].astype(F32)).astype(LOW)
                du_ref[:, cols] = du
                sum_ref[:, cols] = jnp.sum(du.astype(F32), axis=0, keepdims=True)

    return call(
        body,
        "contract_back",
        [shaped((n_rows, hidden), LOW), shaped((1, hidden), F32)],
        [SCALARS, WHOLE, WHOLE, HBM, HBM, HBM],
        [pltpu.VMEM((NP, NZ, kb, width), LOW), pltpu.SemaphoreType.DMA((NP,))],
        [sc, e2, slope] + weight.arrays,
        2 * n_rows * width * hidden,
        32,
    )


def norm_back(grad, source, gain):
    xh, inv = row_stats(source)
    t = grad * gain
    lean = jnp.mean(t, axis=-1, keepdims=True)
    along = jnp.mean(t * xh, axis=-1, keepdims=True)
    back = inv * (t - lean - xh * along)
    return (
        back,
        jnp.sum(grad * xh, axis=0, keepdims=True),
        jnp.sum(grad, axis=0, keepdims=True),
    )


def expand_back(sc, du, middle, d_result, params, weight):
    n_rows, width = middle.shape
    nb = weight.nb

    def body(
        sc_ref, du_ref, h_ref, d_ref, p_ref, own, held, other,
        dh_ref, e_ref, sum_ref, w_ref, acc_ref, sems,
    ):
        r = sc_ref[1]
        weight.start(sc_ref, (own, held, other), weight.rows_first(w_ref), sems)
        acc_ref[...] = jnp.zeros_like(acc_ref)

        @pl.loop(0, NP)
        def _(j):
            part = r ^ j
            wait_for(w_ref.at[part], sems.at[j])
            cols = pl.ds(pl.multiple_of(part * nb, nb), nb)
            acc_ref[...] += nt_dot(du_ref[:, cols], w_ref[part].reshape(width, nb))

        back, gain_sum, shift_sum = norm_back(acc_ref[...], h_ref[...], p_ref[5:6, :])
        dh = d_ref[...] + back
        e1 = dh.astype(LOW)
        dh_ref[...] = dh
        e_ref[...] = e1
        sum_ref[0:1, :] = gain_sum
        sum_ref[1:2, :] = shift_sum
        sum_ref[2:3, :] = jnp.sum(e1.astype(F32), axis=0, keepdims=True)

    return call(
        body,
        "expand_back",
        [
            shaped((n_rows, width), F32),
            shaped((n_rows, width), LOW),
            shaped((3, width), F32),
        ],
        [SCALARS, WHOLE, WHOLE, WHOLE, WHOLE, HBM, HBM, HBM],
        [
            pltpu.VMEM((NP, NZ, weight.kb, nb), LOW),
            pltpu.VMEM((n_rows, width), F32),
            pltpu.SemaphoreType.DMA((NP,)),
        ],
        [sc, du, middle, d_result, params] + weight.arrays,
        2 * n_rows * width * NP * nb,
        40,
    )


def out_back(sc, e1, weight):
    n_rows, width = e1.shape
    nb = weight.nb

    def body(sc_ref, e_ref, own, held, other, d_ref, w_ref, sems):
        weight.start(sc_ref, (own, held, other), weight.flat(w_ref), sems)
        for j in range(NP):
            wait_for(w_ref.at[:, j * nb : (j + 1) * nb], sems.at[j])
        d_ref[...] = nt_dot(e_ref[...], w_ref[...]).astype(LOW)

    return call(
        body,
        "out_back",
        [shaped((n_rows, width), LOW)],
        [SCALARS, WHOLE, HBM, HBM, HBM],
        [pltpu.VMEM((width, width), LOW), pltpu.SemaphoreType.DMA((NP,))],
        [sc, e1] + weight.arrays,
        2 * n_rows * width * width,
        24,
    )[0]


def qkv_back(sc, dq, dk, dv, rows, d_middle, params, weight):
    n_rows, width = rows.shape
    nb = weight.nb
    third = nb // 3

    def body(
        sc_ref, dq_ref, dk_ref, dv_ref, x_ref, d_ref, p_ref, own, held, other,
        gx_ref, sum_ref, w_ref, acc_ref, sems,
    ):
        r = sc_ref[1]
        weight.start(sc_ref, (own, held, other), weight.rows_first(w_ref), sems)
        acc_ref[...] = jnp.zeros_like(acc_ref)

        @pl.loop(0, NP)
        def _(j):
            part = r ^ j
            wait_for(w_ref.at[part], sems.at[j])
            cols = pl.ds(pl.multiple_of(part * third, third), third)
            block = jnp.concatenate([dq_ref[:, cols], dk_ref[:, cols], dv_ref[:, cols]], axis=1)
            acc_ref[...] += nt_dot(block, w_ref[part].reshape(width, nb))

        back, gain_sum, shift_sum = norm_back(acc_ref[...], x_ref[...], p_ref[0:1, :])
        gx_ref[...] = d_ref[...] + back
        sum_ref[0:1, :] = gain_sum
        sum_ref[1:2, :] = shift_sum

    return call(
        body,
        "qkv_back",
        [shaped((n_rows, width), F32), shaped((2, width), F32)],
        [SCALARS] + [WHOLE] * 6 + [HBM] * 3,
        [
            pltpu.VMEM((NP, NZ, weight.kb, nb), LOW),
            pltpu.VMEM((n_rows, width), F32),
            pltpu.SemaphoreType.DMA((NP,)),
        ],
        [sc, dq, dk, dv, rows, d_middle, params] + weight.arrays,
        2 * n_rows * width * NP * nb,
        40,
    )


def grad_call(body, name, sc, args, in_specs, scratch, half, nb, flops, limit):
    out = pl.BlockSpec((2, 1, NZ, half, nb), lambda i, s: (0, i, 0, 0, 0))
    return pl.pallas_call(
        body,
        out_shape=shaped((2, 4, NZ, half, nb), LOW),
        grid_spec=pltpu.PrefetchScalarGridSpec(
            num_scalar_prefetch=1,
            grid=(4,),
            in_specs=in_specs,
            out_specs=out,
            scratch_shapes=scratch,
        ),
        compiler_params=pltpu.CompilerParams(vmem_limit_bytes=limit * MIB),
        cost_estimate=pl.CostEstimate(
            flops=flops,
            bytes_accessed=16 * NZ * half * nb + sum(a.size for a in args),
            transcendentals=0,
        ),
        name=name,
    )(sc, *args)


def grad_columns(sc, pairs, odd, name):
    n_rows, width = pairs[0][0].shape
    kb = width // NZ
    half = kb // 2
    cuts = [[b.shape[1] // NP for b in rights] for _, rights in pairs]
    nb = sum(map(sum, cuts))

    def body(sc_ref, *refs):
        z = sc_ref[0]
        refs = list(refs)
        lefts = [refs.pop(0) for _ in pairs]
        blocks = [[refs.pop(0) for _ in cut] for cut in cuts]
        out_ref = refs.pop(0)

        @pl.when(pl.program_id(0) == 0)
        def _():
            for a_ref, t_ref in zip(lefts, refs):
                for k in range(NZ):
                    cols = pl.ds(pl.multiple_of((z ^ k) * kb, kb), kb)
                    t_ref[k * kb : (k + 1) * kb, :] = a_ref[:, cols].T

        at = 0
        for t_ref, block in zip(refs, blocks):
            right = [b[...] for b in block]
            right = right[0] if len(right) == 1 else jnp.concatenate(right, axis=1)
            cols = slice(at, at + right.shape[1])
            at = cols.stop
            g = nn_dot(t_ref[...], right).astype(LOW)
            for k in range(NZ):
                for h in range(2):
                    row = k * kb + h * half
                    out_ref[h, 0, k, :, cols] = g[row : row + half]

    whole = pl.BlockSpec((n_rows, width), lambda i, s: (0, 0))
    return grad_call(
        body,
        name,
        sc,
        [a for a, _ in pairs] + [b for _, rights in pairs for b in rights],
        [whole] * len(pairs)
        + [
            pl.BlockSpec((n_rows, c), lambda i, s: (0, s[1] ^ (2 * i + odd)))
            for cut in cuts
            for c in cut
        ],
        [pltpu.VMEM((width, n_rows), LOW) for _ in pairs],
        half,
        nb,
        n_rows * width * nb * 8,
        24,
    )


def grad_rows(sc, left, right, odd, name):
    n_rows, hidden = left.shape
    nb = right.shape[1]
    kb = hidden // (NZ * NP)
    half = kb // 2

    def body(sc_ref, a0_ref, a1_ref, a2_ref, a3_ref, b_ref, out_ref):
        block = jnp.concatenate([a[...].T for a in (a0_ref, a1_ref, a2_ref, a3_ref)], axis=0)
        g = nn_dot(block, b_ref[...]).astype(LOW)
        for k in range(NZ):
            for h in range(2):
                row = k * kb + h * half
                out_ref[h, 0, k] = g[row : row + half]

    def part(k):
        return pl.BlockSpec(
            (n_rows, kb), lambda i, s: (0, (s[0] ^ k) * NP + (s[1] ^ (2 * i + odd)))
        )

    return grad_call(
        body,
        name,
        sc,
        [left] * NZ + [right],
        [part(k) for k in range(NZ)] + [pl.BlockSpec((n_rows, nb), lambda i, s: (0, 0))],
        [],
        half,
        nb,
        n_rows * hidden * nb,
        24,
    )


def assemble(sc, sums, flip, shapes, counts, name):
    half, nb = sums[0].shape[2:]
    width = shapes[0][0] * NZ

    def body(sc_ref, *refs):
        r = sc_ref[1]
        outs = refs[2:]
        for core, ref in enumerate(refs[:2]):
            for index in range(4):
                part = r ^ (HELD[flip][index] | core)
                for h in range(2):
                    value = ref[index, h].astype(F32)
                    if counts[0] == 0:
                        row = pl.multiple_of(part * 2 * half + h * half, half)
                        outs[0][pl.ds(row, half), :] = value
                        continue
                    at = 0
                    each = nb // sum(counts)
                    for out, count in zip(outs, counts):
                        for c in range(count):
                            cols = pl.ds(pl.multiple_of(part * each + c * width, each), each)
                            out[h * half : (h + 1) * half, cols] = value[:, at : at + each]
                            at += each

    return call(
        body,
        name,
        [shaped(shape, F32) for shape in shapes],
        [SCALARS, WHOLE, WHOLE],
        [],
        [sc] + list(sums),
        0,
        24,
    )


def per_device(inputs, counts, w_qkv, w_out, w_up, w_down, vectors, cotangent, n_rep):
    links = Links(n_rep)
    seqs, slots, width = inputs.shape
    z = lax.axis_index("shard").astype(jnp.int32)
    r = (lax.axis_index("rep") % NP).astype(jnp.int32)
    sc = jnp.stack([z, r])

    def by_rank(rel):
        return jnp.stack(
            [lax.dynamic_index_in_dim(rel, z ^ i, 0, keepdims=False) for i in range(NZ)]
        )

    v0 = vectors.astype(LOW).reshape(-1, 128)
    v1 = links.zed(v0, 1, "ag_vec_z1")
    v23 = links.zed(jnp.stack([v0, v1]), 2, "ag_vec_z2")
    params = by_rank(jnp.concatenate([v0[None], v1[None], v23]))
    params = params.reshape(12, width).astype(F32)

    kb = w_qkv.shape[0]

    def by_part(w, blocks):
        w = w.astype(LOW).reshape(kb, blocks, NP, -1)
        return w.transpose(2, 0, 1, 3).reshape(NP, kb, -1)

    own_qkv = by_part(w_qkv, 3)
    own_mid = jnp.concatenate([by_part(w_up, 1), by_part(w_out, 1)], axis=2)
    own_down = w_down.astype(LOW).reshape(NP, -1, width)
    qkv_weight = Weight(own_qkv, *gather_parts(links, own_qkv, r, "ag_qkv"))
    mid = [own_mid, *gather_parts(links, own_mid, r, "ag_mid")]
    cut = w_up.shape[1] // NP
    up_weight = Weight(*mid, cols=slice(0, cut))
    out_weight = Weight(*mid, cols=slice(cut, own_mid.shape[2]))
    down_weight = Weight(own_down, *gather_parts(links, own_down, r, "ag_down"))

    valid = lax.broadcasted_iota(jnp.int32, (seqs, slots), 1) < counts[:, None]
    keep_rows = valid.reshape(-1, 1).astype(F32)
    d_result = cotangent.reshape(-1, width) * keep_rows
    e2 = d_result.astype(LOW)
    bias_down_sum = jnp.sum(e2, axis=0, dtype=F32)[None]

    rows = inputs.reshape(-1, width)
    a1, qkv = project_qkv(sc, rows, params, qkv_weight)
    o = attend(counts, qkv, seqs)
    h1, a2 = project_out(sc, o, rows, params, out_weight)
    g, slope = expand(sc, a2, params[8:].reshape(1, -1), up_weight)

    down_send = grad_rows(sc, g, e2, 1, "grad_down_send")
    down_keep = grad_rows(sc, g, e2, 0, "grad_down_keep")
    down_sum = reduce_parts(links, down_keep, down_send, 0, "rs_down")
    du, bias_hidden_sum = contract_back(sc, e2, slope, down_weight)
    up_send = grad_columns(sc, [(a2, [du])], 1, "grad_up_send")
    up_keep = grad_columns(sc, [(a2, [du])], 0, "grad_up_keep")
    up_sum = reduce_parts(links, up_keep, up_send, 1, "rs_up")
    dh1, e1, sums2 = expand_back(sc, du, h1, d_result, params, up_weight)
    d_o = out_back(sc, e1, out_weight)
    dq, dk, dv, bq, bv = attend_back(counts, qkv, d_o, seqs)
    pairs = [(a1, [dq, dk, dv]), (o, [e1])]
    qkv_send = grad_columns(sc, pairs, 1, "grad_qkv_send")
    qkv_keep = grad_columns(sc, pairs, 0, "grad_qkv_keep")
    qkv_sum = reduce_parts(links, qkv_keep, qkv_send, 0, "rs_qkv")
    outputs = contract(sc, g, h1, keep_rows, params, down_weight)
    g_rows, sums1 = qkv_back(sc, dq, dk, dv, rows, dh1, params, qkv_weight)

    vec = jnp.concatenate(
        [
            sums1,
            bq,
            bv,
            sums2[2:3],
            sums2[:2],
            bias_down_sum,
            bias_hidden_sum.reshape(-1, width),
        ]
    ).reshape(NZ, -1, 128)
    bit = 1
    while bit < n_rep:
        vec = vec + links.rep(vec, bit, f"rs_vec_r{bit}")
        bit *= 2
    rel = by_rank(vec)
    rel = rel[:2] + links.zed(rel[2:], 2, "rs_vec_z2")
    grad_vectors = (rel[0] + links.zed(rel[1], 1, "rs_vec_z1")).reshape(-1)

    grad_qkv, grad_out = assemble(sc, qkv_sum, 0, [w_qkv.shape, w_out.shape], [3, 1], "sum_qkv")
    (grad_up,) = assemble(sc, up_sum, 1, [w_up.shape], [1], "sum_up")
    (grad_down,) = assemble(sc, down_sum, 0, [w_down.shape], [0], "sum_down")
    return (
        outputs.reshape(seqs, slots, width),
        g_rows.reshape(seqs, slots, width),
        grad_qkv,
        grad_out,
        grad_up,
        grad_down,
        grad_vectors,
    )


def solution(mesh):
    batch = P(("shard", "rep"), None, None)
    weight = P("shard", None)
    return jax.shard_map(
        functools.partial(per_device, n_rep=mesh.shape["rep"]),
        mesh=mesh,
        in_specs=(batch, P(("shard", "rep")), weight, weight, weight, weight, P("shard"), batch),
        out_specs=(batch, batch, weight, weight, weight, weight, P("shard")),
        check_vma=False,
    )
```
